32 devices in a mesh: member: 8 (over z, x), dp: 4 (over y, core).
Axes of the slice: x: 2, y: 2, z: 4, core: 2. Of those that a mesh axis runs over, the one named last changes fastest.
Arguments:
- feature_pool: bfloat16 [2048, 256], P('dp'), may hold values from -6 to 6
- labels: int32 [2048], P('dp'), may hold values from 0 to 9
- sample_rows: int32 [1024], P('dp'), may hold values from 0 to 511
- noise_variance: float32 [10], replicated, may hold values from 160 to 640
- first_weight: bfloat16 [16, 256, 2048], P('member', None, 'dp'), may hold values from -6 to 6
- middle_weight: bfloat16 [16, 2048, 2048], P('member', 'dp'), may hold values from -6 to 6
- last_weight: bfloat16 [16, 2048, 10], P('member', 'dp'), may hold values from -6 to 6
Outputs:
- new_first: bfloat16 [16, 256, 2048], P('member', None, 'dp')
- new_middle: bfloat16 [16, 2048, 2048], P('member', 'dp')
- new_last: bfloat16 [16, 2048, 10], P('member', 'dp')
The draws below stay inside these ranges and needn't reach their ends.
Inputs may be any that keep to these rules, and one draw needn't show every extreme that they name: Sample i reads pool row (i // 256) * 512 + sample_rows[i]. `labels`: class index of each pool row.
All inputs are finite; a program needn't handle non-finite values.
Results may differ from the reference program's by a relative error of at most 0.013.
Values may be sent and summed in bfloat16 or wider, within the bound.
No kernel may reach another device: no remote copies, remote signals or barrier semaphores. Data moves between devices by JAX's collectives and lax.ppermute only.
A program may use at most 128 MiB of HBM per device.

```python
import math
import jax
import jax.numpy as jnp
from jax import lax

F_IN = 256
H = 2048
C = 10
SAMP_DEV = 256
POOL_DEV = 512
MEMBERS = 16
SAMPLES = 1024
POOL = 2048


def plant(array, own_key, low, top_value):
    longest = array.shape.index(max(array.shape))
    spots = []
    for shift in (0, 1):
        where = [jax.random.randint(jax.random.fold_in(own_key, axis), (), 0, length) for axis, length in enumerate(array.shape)]
        where[longest] = (where[longest] + shift) % array.shape[longest]
        spots.append(tuple(where))
    return array.at[spots[0]].set(low).at[spots[1]].set(top_value)


def steps_of(own_key, dims, shards, least, high):
    def one(dim, parts):
        steps = jax.random.uniform(jax.random.fold_in(jax.random.fold_in(own_key, 6), dim), (parts,), jnp.float32, least / len(shards), high / len(shards))
        return jnp.repeat(jnp.exp(steps), dims[dim] // parts).reshape((-1,) + (1,) * (len(dims) - dim - 1))

    gain = one(*shards[0])
    for cut in shards[1:]:
        gain = gain * one(*cut)
    return gain


def scatter_about(rng, shape, scale, bound, pieces=(), kind=jnp.bfloat16):
    drawn = scale * jax.random.normal(rng, shape, jnp.float32)
    if pieces:
        drawn = drawn * steps_of(rng, shape, pieces, -0.22, 0.18)
    return jnp.clip(drawn, -bound, bound).astype(kind)


def setup_inputs(seed: int = 0) -> dict:
    streams_of = jax.random.split(jax.random.key(seed), 8)
    return {
        "feature_pool": scatter_about(streams_of[0], (POOL, F_IN), 1.0, 6.0, ((0, 4),)),
        "labels": plant(jax.random.randint(streams_of[1], (POOL,), 0, C), jax.random.fold_in(streams_of[1], 1), 0, C - 1).astype(jnp.int32),
        "sample_rows": plant(jax.random.randint(streams_of[2], (SAMPLES,), 0, POOL_DEV), jax.random.fold_in(streams_of[2], 1), 0, POOL_DEV - 1).astype(jnp.int32),
        "noise_variance": jnp.clip(jnp.exp(jax.random.uniform(streams_of[3], (C,), jnp.float32, math.log(160.0), math.log(640.0))), 160.0, 640.0),
        "first_weight": scatter_about(streams_of[4], (MEMBERS, F_IN, H), 1.0, 6.0, ((0, 8), (2, 4))),
        "middle_weight": scatter_about(streams_of[5], (MEMBERS, H, H), 1.0, 6.0, ((0, 8), (1, 4))),
        "last_weight": scatter_about(streams_of[6], (MEMBERS, H, C), 1.0, 6.0, ((0, 8), (1, 4))),
    }


precise = lax.Precision.HIGHEST

def member_outputs(inputs, first, middle, last):
    hidden_one = jnp.tanh(jnp.dot(inputs.astype(jnp.float32), first.astype(jnp.float32), preferred_element_type=jnp.float32) * F_IN ** (-0.5)).astype(jnp.bfloat16)
    hidden_two = jnp.tanh(jnp.dot(hidden_one.astype(jnp.float32), middle.astype(jnp.float32), preferred_element_type=jnp.float32) * H ** (-0.5)).astype(jnp.bfloat16)
    return jnp.dot(hidden_two.astype(jnp.float32), last.astype(jnp.float32), preferred_element_type=jnp.float32) * H ** (-0.5)

def update_block(block, mixing):
    values = block.astype(jnp.float32)
    anomaly = values - lax.optimization_barrier(jnp.mean(values, axis=0, keepdims=True))
    return (values + jnp.dot(mixing.T, anomaly, precision=precise)).astype(jnp.bfloat16)

def update_tensor(tensor, mixing):
    moved = jnp.moveaxis(tensor, 1, 0)

    def one_row(block):
        return update_block(block, mixing)
    done = lax.map(one_row, moved)
    return jnp.moveaxis(done, 0, 1)

def reference(feature_pool, labels, sample_rows, noise_variance, first_weight, middle_weight, last_weight):
    positions = jnp.arange(SAMPLES, dtype=jnp.int32)
    rows = (positions // SAMP_DEV * POOL_DEV + sample_rows).astype(jnp.int32)
    inputs = feature_pool[rows]
    classes = labels[rows]
    target = (classes[:, None] == jnp.arange(C, dtype=jnp.int32)[None, :]).astype(jnp.float32)
    whiten = 1.0 / jnp.sqrt(noise_variance)

    def forward(weights):
        return member_outputs(inputs, weights[0], weights[1], weights[2])
    outputs = lax.map(forward, (first_weight, middle_weight, last_weight))
    scaled = (outputs * whiten).reshape(MEMBERS, SAMPLES * C)
    observed = (target * whiten).reshape(SAMPLES * C)
    center = lax.optimization_barrier(jnp.mean(scaled, axis=0))
    anomaly = scaled - center
    gram_matrix = jnp.dot(anomaly, anomaly.T, precision=precise)
    drive = jnp.dot(anomaly, observed - center, precision=precise)
    system = gram_matrix + MEMBERS * jnp.eye(MEMBERS, dtype=jnp.float32)
    factor = jnp.linalg.cholesky(system)
    mixing = jax.scipy.linalg.cho_solve((factor, True), drive[:, None] - gram_matrix)
    return (update_tensor(first_weight, mixing), update_tensor(middle_weight, mixing), update_tensor(last_weight, mixing))
```

```python
import jax
import jax.numpy as jnp
from jax import lax
from jax.experimental import pallas as pl
from jax.experimental.pallas import tpu as pltpu
from jax.sharding import PartitionSpec as P


GROUP = 16
WIDEST = 256
precise = lax.Precision.HIGHEST


def swap(value, axis, size, k):
    return lax.ppermute(value, axis, [(i, i ^ k) for i in range(size)])


def bits_of(size):
    return [1 << b for b in range(size.bit_length() - 1)]


def gather_xor(value, axis, size, bits):
    stack, order = value[None], [0]
    for bit in bits:
        stack = jnp.concatenate([stack, swap(stack, axis, size, bit)], axis=0)
        order = order + [o ^ bit for o in order]
    return stack, order


def gather_members(value, size):
    have = [value]
    bits = bits_of(size)
    groups = [bits[:1]] + [bits[i : i + 2] for i in range(1, len(bits), 2)]
    for group in groups:
        stack = jnp.concatenate(have, axis=0)
        count = len(have)
        fresh = []
        for step in range(1, 1 << len(group)):
            k = step * group[0]
            got = swap(stack, "member", size, k)
            fresh += jnp.split(got, count, axis=0)
        have = have + fresh
    return have


def gather_blocks(place, array, reads, shapes, steps):
    counts = [len(read) for read in reads]

    def kernel(place_ref, *refs):
        ins, outs = refs[: sum(counts)], refs[sum(counts) :]
        at = 0
        for out, count in zip(outs, counts):
            left = 0
            for ref in ins[at : at + count]:
                value = ref[...]
                value = value.reshape([n for i, n in enumerate(value.shape) if i not in drop])
                out[..., left : left + value.shape[-1]] = value
                left += value.shape[-1]
            at += count

    drop, out_specs = shapes[0][2], [
        pl.BlockSpec(block, index) for (_, (block, index), _) in shapes
    ]
    flat = [pl.BlockSpec(block, index) for read in reads for block, index in read]
    return pl.pallas_call(
        kernel,
        grid_spec=pltpu.PrefetchScalarGridSpec(
            num_scalar_prefetch=1, grid=(steps,), in_specs=flat, out_specs=out_specs
        ),
        out_shape=[jax.ShapeDtypeStruct(shape, array.dtype) for (shape, _, _) in shapes],
    )(place, *[array] * len(flat))


def join_blocks(place, shape, pieces, start, into=None):
    members, count = len(pieces), pieces[0].shape[1]
    slots, columns = pieces[0].shape[0], pieces[0].shape[2]
    extra = [] if into is None else [into]

    def kernel(place_ref, *refs):
        out = refs[-1]
        for k in range(members):
            @pl.when(pl.program_id(0) == k)
            def _():
                out[:, 0] = refs[k][...]

    return pl.pallas_call(
        kernel,
        grid_spec=pltpu.PrefetchScalarGridSpec(
            num_scalar_prefetch=1,
            grid=(members,),
            in_specs=[pl.BlockSpec(p.shape, lambda i, place_ref: (0, 0, 0)) for p in pieces]
            + [pl.BlockSpec(memory_space=pl.ANY)] * len(extra),
            out_specs=pl.BlockSpec(
                (slots, 1, count, columns),
                lambda i, place_ref: (0, place_ref[0] ^ i, start // count, 0),
            ),
        ),
        out_shape=jax.ShapeDtypeStruct(shape, pieces[0].dtype),
        input_output_aliases={} if into is None else {1 + members: 0},
    )(place, *pieces, *extra)


def spread(matrix, rows):
    n = matrix.shape[0]
    wide = n * rows
    pick = (
        lax.broadcasted_iota(jnp.int32, (wide, n), 0) // rows
        == lax.broadcasted_iota(jnp.int32, (wide, n), 1)
    ).astype(jnp.bfloat16)
    tall = jnp.dot(pick, matrix, preferred_element_type=jnp.float32).astype(jnp.bfloat16)
    full = lax.dot_general(
        tall, pick, (((1,), (1,)), ((), ())), preferred_element_type=jnp.float32
    )
    same = (
        lax.broadcasted_iota(jnp.int32, (wide, wide), 0) % rows
        == lax.broadcasted_iota(jnp.int32, (wide, wide), 1) % rows
    )
    return jnp.where(same, full, 0.0).astype(jnp.bfloat16)


def update_pieces(weights, pieces, block):
    count = len(pieces)
    slots, rows, columns = pieces[0].shape
    wide = count * slots * GROUP

    def kernel(weights_ref, *refs):
        ins, outs = refs[:count], refs[count : 2 * count]
        upper_ref, lower_ref = refs[2 * count :]

        @pl.when(pl.program_id(0) == 0)
        def _():
            upper = weights_ref[...].astype(jnp.bfloat16)
            lower = (weights_ref[...] - upper.astype(jnp.float32)).astype(jnp.bfloat16)
            upper_ref[...] = spread(upper, GROUP)
            lower_ref[...] = spread(lower, GROUP)

        for first in range(0, rows, GROUP):
            data = jnp.concatenate(
                [ref[s, first : first + GROUP, :] for ref in ins for s in range(slots)], axis=0
            )
            total = jnp.dot(upper_ref[...], data, preferred_element_type=jnp.float32)
            total += jnp.dot(lower_ref[...], data, preferred_element_type=jnp.float32)
            total = total.astype(jnp.bfloat16)
            for i, ref in enumerate(outs):
                for s in range(slots):
                    at = (i * slots + s) * GROUP
                    ref[s, first : first + GROUP, :] = total[at : at + GROUP]

    spec = pl.BlockSpec((slots, rows, block), lambda i: (0, 0, i))
    return pl.pallas_call(
        kernel,
        grid=(columns // block,),
        in_specs=[pl.BlockSpec(weights.shape, lambda i: (0, 0))] + [spec] * count,
        out_specs=[spec] * count,
        out_shape=[jax.ShapeDtypeStruct(pieces[0].shape, pieces[0].dtype)] * count,
        scratch_shapes=[pltpu.VMEM((wide, wide), jnp.bfloat16)] * 2,
    )(weights, *pieces)


def layer_one(inputs, weights, scale):
    count, features, width = weights.shape
    rows = inputs.shape[0]

    def kernel(inputs_ref, weights_ref, out_ref):
        product = jnp.dot(inputs_ref[...], weights_ref[0], preferred_element_type=jnp.float32)
        out_ref[...] = jnp.tanh(product * scale).astype(jnp.bfloat16)

    return pl.pallas_call(
        kernel,
        grid=(count,),
        in_specs=[
            pl.BlockSpec((rows, features), lambda i: (0, 0)),
            pl.BlockSpec((1, features, width), lambda i: (i, 0, 0)),
        ],
        out_specs=pl.BlockSpec((rows, width), lambda i: (0, i)),
        out_shape=jax.ShapeDtypeStruct((rows, count * width), jnp.bfloat16),
        name="layer_one",
    )(inputs, weights)


def layers_after(hidden, pieces, last, scale, block):
    samples = hidden.shape[0]
    width, columns = pieces[0].shape
    classes = last.shape[0]
    count = len(pieces)

    def kernel(hidden_ref, last_ref, *refs):
        out_ref = refs[count]
        total = None
        for i in range(count):
            term = jnp.dot(
                hidden_ref[:, i * width : (i + 1) * width],
                refs[i][...],
                preferred_element_type=jnp.float32,
            )
            total = term if total is None else total + term
        hidden_two = jnp.tanh(total * scale).astype(jnp.bfloat16)
        out = lax.dot_general(
            last_ref[...], hidden_two, (((1,), (1,)), ((), ())),
            preferred_element_type=jnp.float32,
        )
        out_ref[...] = out * scale

    return pl.pallas_call(
        kernel,
        grid=(samples // block,),
        in_specs=[
            pl.BlockSpec((block, count * width), lambda i: (i, 0)),
            pl.BlockSpec((classes, columns), lambda i: (0, 0)),
        ]
        + [pl.BlockSpec((width, columns), lambda i: (0, 0))] * count,
        out_specs=pl.BlockSpec((classes, block), lambda i: (0, i)),
        out_shape=jax.ShapeDtypeStruct((classes, samples), jnp.float32),
        name="layers_after",
    )(hidden, last, *pieces)


def forward(inputs, first_weight, middle_weight, last_weight, size, place):
    slots, features, width = first_weight.shape
    parts = size // slots
    units = middle_weight.shape[2]
    here = lax.axis_index("dp")
    y = here // parts
    samples = inputs.shape[0]

    steps = 4
    tall = width // steps

    def column_block(d, e):
        dy, dc = d // parts, d % parts

        def index(i, place_ref):
            y, c = place_ref[1] // parts, place_ref[1] % parts
            return (y ^ dy, i, (y ^ dy ^ e) * parts + (c ^ dc))

        return (1, tall, width), index

    middle_out = gather_blocks(
        place, middle_weight,
        [[column_block(d, e) for e in range(slots)] for d in range(size)],
        [
            ((width, slots * width), ((tall, slots * width), lambda i, place_ref: (i, 0)), (0,))
            for _ in range(size)
        ],
        steps,
    )
    middle_at = [middle_out[0]] + [swap(middle_out[d], "dp", size, d) for d in range(1, size)]

    def slot_of(array, dy):
        return lax.dynamic_index_in_dim(array, y ^ dy, 0, keepdims=False)

    every_input, order = gather_xor(inputs, "dp", size, bits_of(size)[::-1])
    every_input = every_input.reshape(size * samples, features)
    first_mine = jnp.stack(
        [slot_of(first_weight, 0)]
        + [swap(slot_of(first_weight, dy), "dp", size, dy * parts) for dy in range(1, slots)]
    )
    first_all, first_order = gather_xor(first_mine, "dp", size, bits_of(parts))
    last_flipped = jnp.transpose(last_weight, (0, 2, 1))
    last_mine = jnp.concatenate(
        [slot_of(last_flipped, 0)]
        + [swap(slot_of(last_flipped, dy), "dp", size, dy * parts) for dy in range(1, slots)],
        axis=1,
    )
    hidden_one = layer_one(
        every_input, first_all.reshape(size, features, width), features ** (-0.5)
    )
    middle_order = [dy * parts + dc for dc in first_order for dy in range(slots)]
    outputs = layers_after(
        hidden_one, [middle_at[d] for d in middle_order], last_mine, units ** (-0.5), samples
    )
    received = [None] * size
    for spot, d in enumerate(order):
        block = outputs[:, spot * samples : (spot + 1) * samples]
        received[d] = block if d == 0 else swap(block, "dp", size, d)
    by_slot = jnp.stack(
        [sum(received[dy * parts + dc] for dc in range(parts)) for dy in range(slots)]
    )
    return jnp.stack(
        [lax.dynamic_index_in_dim(by_slot, y ^ s, 0, keepdims=False) for s in range(slots)]
    )


def mixing_of(every, observed, size):
    ensemble = every.shape[0]
    center = jnp.mean(every, axis=0)
    anomaly = (every - center).reshape(ensemble, -1)
    rest = (observed - center).reshape(1, -1)
    both = lax.dot_general(
        anomaly,
        jnp.concatenate([anomaly, rest], axis=0),
        (((1,), (1,)), ((), ())),
        precision=precise,
        preferred_element_type=jnp.float32,
    )
    for bit in bits_of(size):
        both = both + swap(both, "dp", size, bit)
    gram_matrix, drive = both[:, :ensemble], both[:, ensemble:]
    system = gram_matrix + ensemble * jnp.eye(ensemble, dtype=jnp.float32)
    factor = jnp.linalg.cholesky(system)
    return jax.scipy.linalg.cho_solve((factor, True), drive - gram_matrix)


def exchanged(pieces, members):
    out = [pieces[0]] + [None] * (members - 1)
    for k in far_first(members):
        out[k] = swap(pieces[k], "member", members, k)
    return out


def far_first(members):
    return list(range(members - 1, 0, -1))


def on_device(
    members, size,
    feature_pool, labels, sample_rows, noise_variance, first_weight, middle_weight, last_weight,
):
    slots = first_weight.shape[0]
    classes_total = noise_variance.shape[0]
    ensemble = members * slots
    here = lax.axis_index("member")
    place = jnp.stack([here, lax.axis_index("dp")]).astype(jnp.int32)
    whiten = 1.0 / jnp.sqrt(noise_variance)
    inputs = feature_pool[sample_rows]
    classes = labels[sample_rows]
    target = (
        classes[None, :] == jnp.arange(classes_total, dtype=jnp.int32)[:, None]
    ).astype(jnp.float32)
    observed = target * whiten[:, None]

    def blocks(array):
        return array.reshape((slots, members, array.shape[1] // members) + array.shape[2:])

    first_blocks, middle_blocks = blocks(first_weight), blocks(middle_weight)
    rows = middle_blocks.shape[2]
    fits = rows % GROUP == 0 and first_blocks.shape[2] % GROUP == 0 and ensemble * GROUP <= WIDEST
    scaled_of = lambda: (
        forward(inputs, first_weight, middle_weight, last_weight, size, place)
        * whiten[None, :, None]
    )
    if not fits:
        every = jnp.concatenate(gather_members(scaled_of(), members), axis=0)
        return plain_update(
            mixing_of(every, observed, size), members, first_weight, middle_weight, last_weight
        )

    last_flat = jnp.transpose(blocks(last_weight), (1, 0, 3, 2)).reshape(members, slots, -1)
    early = rows * 3 // 4 // GROUP * GROUP

    def cut(array, start, count, steps):
        columns = array.shape[3]
        wide = columns // steps

        def read(k):
            return (
                (slots, 1, count, wide),
                lambda i, place_ref: (0, place_ref[0] ^ k, start // count, i),
            )

        out = ((slots, count, columns), ((slots, count, wide), lambda i, place_ref: (0, 0, i)), (1,))
        return gather_blocks(
            place, array, [[read(k)] for k in range(members)], [out] * members, steps
        )

    middle_early = exchanged(cut(middle_blocks, 0, early, 4), members)
    late_cut = cut(middle_blocks, early, rows - early, 4)
    first_in = exchanged(cut(first_blocks, 0, first_blocks.shape[2], 1), members)
    last_in = exchanged(
        [lax.dynamic_index_in_dim(last_flat, here ^ k, 0, keepdims=False) for k in range(members)],
        members,
    )
    every = jnp.concatenate(gather_members(scaled_of(), members), axis=0)
    middle_late = exchanged(late_cut, members)

    mixing = mixing_of(every, observed, size)
    weights = (
        jnp.eye(ensemble, dtype=jnp.float32)
        + mixing
        - jnp.mean(mixing, axis=0, keepdims=True)
    ).T

    block = middle_weight.shape[2] // 4
    early_back = exchanged(update_pieces(weights, middle_early, block), members)
    first_back = exchanged(update_pieces(weights, first_in, first_weight.shape[2]), members)
    last_stack = jnp.concatenate(last_in, axis=0).astype(jnp.float32)
    last_new = jnp.dot(weights, last_stack, precision=precise).astype(jnp.bfloat16)
    last_back = exchanged(jnp.split(last_new, members, axis=0), members)
    late_back = exchanged(update_pieces(weights, middle_late, block), members)

    new_first = join_blocks(place, first_blocks.shape, first_back, 0)
    new_middle = join_blocks(place, middle_blocks.shape, early_back, 0)
    new_middle = join_blocks(place, middle_blocks.shape, late_back, early, new_middle)
    last_whole = jnp.zeros((members, slots, last_new.shape[1]), jnp.bfloat16)
    for k in range(members):
        last_whole = lax.dynamic_update_slice(last_whole, last_back[k][None], (here ^ k, 0, 0))
    new_last = last_whole.reshape(members, slots, classes_total, -1)
    new_last = jnp.transpose(new_last, (1, 0, 3, 2)).reshape(last_weight.shape)
    return (
        new_first.reshape(first_weight.shape),
        new_middle.reshape(middle_weight.shape),
        new_last,
    )


def plain_update(mixing, members, first_weight, middle_weight, last_weight):
    slots = first_weight.shape[0]
    ensemble = members * slots
    member = jnp.arange(ensemble, dtype=jnp.int32)
    spot = (member // slots ^ lax.axis_index("member")) * slots + member % slots
    mixing = mixing[spot][:, spot]
    weights = (
        jnp.eye(ensemble, dtype=jnp.float32)
        + mixing
        - jnp.mean(mixing, axis=0, keepdims=True)
    ).T
    upper = weights.astype(jnp.bfloat16)
    lower = (weights - upper.astype(jnp.float32)).astype(jnp.bfloat16)

    def renew(array):
        piece = lax.all_to_all(array, "member", split_axis=1, concat_axis=0, tiled=True)
        flat = piece.reshape(ensemble, -1)
        new = jnp.dot(upper, flat, preferred_element_type=jnp.float32)
        new += jnp.dot(lower, flat, preferred_element_type=jnp.float32)
        new = new.astype(jnp.bfloat16).reshape(piece.shape)
        return lax.all_to_all(new, "member", split_axis=0, concat_axis=1, tiled=True)

    return renew(first_weight), renew(middle_weight), renew(last_weight)


def solution(mesh):
    members, size = mesh.shape["member"], mesh.shape["dp"]
    in_specs = (
        P("dp", None),
        P("dp"),
        P("dp"),
        P(),
        P("member", None, "dp"),
        P("member", "dp", None),
        P("member", "dp", None),
    )
    out_specs = (P("member", None, "dp"), P("member", "dp", None), P("member", "dp", None))

    def step(*arrays):
        return on_device(members, size, *arrays)

    def run(*arrays):
        mapped = jax.shard_map(
            step, mesh=mesh, in_specs=in_specs, out_specs=out_specs, check_vma=False
        )
        return mapped(*arrays)

    return run
```

```python
import jax
import jax.numpy as jnp
from jax import lax
from jax.experimental import pallas as pl
from jax.experimental.pallas import tpu as pltpu
from jax.sharding import PartitionSpec as P


GROUP = 16
WIDEST = 256
precise = lax.Precision.HIGHEST
MEMBER, DP = "member", "dp"


def swap(value, axis, size, k):
    return lax.ppermute(value, axis, [(i, i ^ k) for i in range(size)])


def launch(kernel, **settings):
    return pl.pallas_call(kernel, **settings)


def bits_of(size):
    return [1 << b for b in range(size.bit_length() - 1)]


def gather_members(value, size):
    have = [value]
    bits = bits_of(size)
    groups = [bits[:1]] + [bits[i : i + 2] for i in range(1, len(bits), 2)]
    for group in groups:
        stack = jnp.concatenate(have, axis=0) if len(have) > 1 else have[0]
        ks = [step * group[0] for step in range(1, 1 << len(group))]
        have = have + [swap(stack, MEMBER, size, k) for k in ks]
    return have


def copies(place, sources, plan, out_shapes, into=()):
    count, kept, results = len(sources), len(into), len(out_shapes)
    shapes = plan(None, None, None)
    total = len(shapes)

    def kernel(place_ref, *refs):
        ins, outs = refs[:count], refs[count + kept : count + kept + results]
        stage, sems = refs[-total - 1 : -1], refs[-1]
        items = [
            (
                [
                    pltpu.make_async_copy(a, stage[i].at[at], sems.at[0, i, j])
                    for j, (a, at) in enumerate(inward)
                ],
                [
                    pltpu.make_async_copy(stage[i].at[at], b, sems.at[1, i, j])
                    for j, (at, b) in enumerate(outward)
                ],
            )
            for i, (inward, outward) in enumerate(plan(place_ref, ins, outs))
        ]
        for inward, _ in items:
            for copy in inward:
                copy.start()
        for inward, outward in items:
            for copy in inward:
                copy.wait()
            for copy in outward:
                copy.start()
        for _, outward in items:
            for copy in outward:
                copy.wait()

    anywhere = pl.BlockSpec(memory_space=pl.ANY)
    return launch(
        kernel,
        in_specs=[pl.BlockSpec(memory_space=pltpu.SMEM)] + [anywhere] * (count + kept),
        out_specs=[anywhere] * results,
        out_shape=out_shapes,
        scratch_shapes=[pltpu.VMEM(shape, jnp.bfloat16) for shape in shapes]
        + [pltpu.SemaphoreType.DMA((2, total, 8))],
        input_output_aliases={1 + count + i: i for i in range(kept)},
    )(place, *sources, *into)


def views(middle, first, k, place_ref, early, late):
    slots, _, rows, _ = middle.shape
    _, _, tall, wide = first.shape
    block, half, found, at = place_ref[0] ^ k, rows // 2, [], 0
    for wanted, start in ((late, half), (early, 0)):
        for s in range(slots if wanted else 0):
            found.append((pl.ds(at, half), middle.at[s, block, start : start + half]))
            at += half
    for s in range(slots if early else 0):
        for h in range(tall // GROUP):
            left = (s * (tall // GROUP) + h) * wide
            found.append(
                (
                    (pl.ds(at, GROUP), pl.ds(left, wide)),
                    first.at[s, block, h * GROUP : (h + 1) * GROUP],
                )
            )
    return found


def piece_shape(middle, early, late):
    slots, _, rows, columns = middle.shape
    return (slots * (rows // 2) * (early + late) + GROUP * early, columns)


def cut_pieces(place, middle, first, wanted):
    shapes = [piece_shape(middle, early, late) for _, early, late in wanted]

    def plan(place_ref, ins, outs):
        if place_ref is None:
            return shapes
        return [
            (
                [(b, at) for at, b in views(*ins, k, place_ref, early, late)],
                [(slice(None), out)],
            )
            for (k, early, late), out in zip(wanted, outs)
        ]

    return list(
        copies(
            place, [middle, first], plan,
            [jax.ShapeDtypeStruct(shape, middle.dtype) for shape in shapes],
        )
    )


def join_early(place, middle_shape, first_shape, pieces):
    def plan(place_ref, ins, outs):
        if place_ref is None:
            return [piece.shape for piece in pieces.values()]
        return [
            ([(ref, slice(None))], views(*outs, k, place_ref, 1, 0)) for k, ref in zip(pieces, ins)
        ]

    shapes = [jax.ShapeDtypeStruct(shape, jnp.bfloat16) for shape in (middle_shape, first_shape)]
    return copies(place, list(pieces.values()), plan, shapes)


def join_late(place, middle, first, pieces):
    def plan(place_ref, ins, outs):
        if place_ref is None:
            return [piece.shape for piece in pieces.values()]
        return [
            ([(ref, slice(None))], views(outs[0], first, k, place_ref, 0, 1))
            for k, ref in zip(pieces, ins)
        ]

    shape = jax.ShapeDtypeStruct(middle.shape, middle.dtype)
    return copies(place, list(pieces.values()), plan, [shape], [middle])[0]


def spread(matrix, rows):
    n = matrix.shape[0]
    wide = n * rows
    pick = (
        lax.broadcasted_iota(jnp.int32, (wide, n), 0) // rows
        == lax.broadcasted_iota(jnp.int32, (wide, n), 1)
    ).astype(jnp.bfloat16)
    tall = lax.dot_general(
        pick, matrix, (((1,), (1,)), ((), ())), preferred_element_type=jnp.float32
    ).astype(jnp.bfloat16)
    full = lax.dot_general(
        tall, pick, (((1,), (1,)), ((), ())), preferred_element_type=jnp.float32
    )
    same = (
        lax.broadcasted_iota(jnp.int32, (wide, wide), 0) % rows
        == lax.broadcasted_iota(jnp.int32, (wide, wide), 1) % rows
    )
    return jnp.where(same, full, 0.0).astype(jnp.bfloat16)


def update_pieces(weights, pieces, slots, rows, block, strips=()):
    count, extra = len(pieces), len(strips)
    columns = pieces[0][0].shape[1]
    wide = count * slots * GROUP
    tall = slots * rows + (GROUP if strips else 0)
    halves = columns // block // slots

    def kernel(weights_ref, *refs):
        ins, refs = refs[:count], refs[count:]
        strip_refs, refs = refs[:extra], refs[extra:]
        outs, (upper_ref, lower_ref) = refs[:count], refs[count:]
        step = pl.program_id(0)

        @pl.when(step == 0)
        def _():
            upper = weights_ref[...].astype(jnp.bfloat16)
            lower = (weights_ref[...] - upper.astype(jnp.float32)).astype(jnp.bfloat16)
            upper_ref[...] = spread(upper, GROUP)
            lower_ref[...] = spread(lower, GROUP)

        def renewed(data):
            data = jnp.concatenate(data, axis=0)
            total = jnp.dot(upper_ref[...], data, preferred_element_type=jnp.float32)
            total += jnp.dot(lower_ref[...], data, preferred_element_type=jnp.float32)
            return total.reshape(count, slots, GROUP, block)

        for first in range(0, rows, GROUP):
            total = renewed(
                [
                    ref[s * rows + first : s * rows + first + GROUP, :]
                    for ref in ins
                    for s in range(slots)
                ]
            ).astype(jnp.bfloat16)
            for i, ref in enumerate(outs):
                for s in range(slots):
                    ref[s * rows + first : s * rows + first + GROUP, :] = total[i, s]
        if strips:
            half = step % halves
            total = renewed(
                [
                    ref[:, pl.ds(pl.multiple_of((s * halves + half) * block, block), block)]
                    for ref in strip_refs
                    for s in range(slots)
                ]
            )
            for i, ref in enumerate(outs):
                mine = total[i, 0]
                for s in range(1, slots):
                    mine = jnp.where(step // halves == s, total[i, s], mine)
                ref[slots * rows : tall, :] = mine.astype(jnp.bfloat16)

    return launch(
        kernel,
        grid=(columns // block,),
        in_specs=[pl.BlockSpec(weights.shape, lambda i: (0, 0))]
        + [pl.BlockSpec((slots * rows, block), lambda i, at=at: (at, i)) for _, at in pieces]
        + [pl.BlockSpec((GROUP, columns), lambda i, at=at: (at, 0)) for _, at in strips],
        out_specs=[pl.BlockSpec((tall, block), lambda i: (0, i))] * count,
        out_shape=[jax.ShapeDtypeStruct((tall, columns), jnp.bfloat16)] * count,
        scratch_shapes=[pltpu.VMEM((wide, wide), jnp.bfloat16)] * 2,
    )(weights, *[array for array, _ in pieces], *[array for array, _ in strips])


def layer_one(inputs, weights, scale, steps):
    rows, features = inputs[0].shape
    width = weights[0].shape[1]
    count, blocks = len(inputs), len(weights)
    tall = rows // steps

    def kernel(*refs):
        out_ref = refs[-1]
        data = jnp.concatenate([ref[...] for ref in refs[:count]], axis=0)
        for j in range(blocks):
            product = jnp.dot(data, refs[count + j][...], preferred_element_type=jnp.float32)
            hidden = jnp.tanh(product * scale).astype(jnp.bfloat16)
            for i in range(count):
                out_ref[i, :, j * width : (j + 1) * width] = hidden[i * tall : (i + 1) * tall]

    return launch(
        kernel,
        grid=(steps,),
        in_specs=[pl.BlockSpec((tall, features), lambda i: (i, 0))] * count
        + [pl.BlockSpec((features, width), lambda i: (0, 0))] * blocks,
        out_specs=pl.BlockSpec((count, tall, blocks * width), lambda i: (0, i, 0)),
        out_shape=jax.ShapeDtypeStruct((count, rows, blocks * width), jnp.bfloat16),
    )(*inputs, *weights)


def layer_two(place, hidden, own, pieces):
    groups, rows, _ = hidden.shape
    width, columns = pieces[0][1].shape
    array, maps = own
    count, own_count = len(pieces), len(maps)

    def kernel(place_ref, *refs):
        hidden_refs, refs = refs[: count + 1], refs[count + 1 :]
        own_refs, piece_refs, out_ref = refs[:own_count], refs[own_count:-1], refs[-1]
        value = jnp.concatenate(
            [
                jnp.dot(hidden_refs[0][0], ref[0], preferred_element_type=jnp.float32)
                for ref in own_refs
            ],
            axis=1,
        )
        for hidden_ref, ref in zip(hidden_refs[1:], piece_refs):
            value += jnp.dot(hidden_ref[0], ref[...], preferred_element_type=jnp.float32)
        out_ref[0] = value

    def column(at):
        return pl.BlockSpec((1, rows, width), lambda i, place_ref: (i, 0, at))

    return launch(
        kernel,
        grid_spec=pltpu.PrefetchScalarGridSpec(
            num_scalar_prefetch=1,
            grid=(groups,),
            in_specs=[column(0)] + [column(at) for at, _ in pieces]
            + [pl.BlockSpec((1, width, columns // own_count), index) for index in maps]
            + [pl.BlockSpec((width, columns), lambda i, place_ref: (0, 0))] * count,
            out_specs=pl.BlockSpec((1, rows, columns), lambda i, place_ref: (i, 0, 0)),
        ),
        out_shape=jax.ShapeDtypeStruct((groups, rows, columns), jnp.float32),
    )(place, *[hidden] * (count + 1), *[array] * own_count, *[value for _, value in pieces])


def layers_after(hidden, piece, total, last, scales, scale):
    groups, rows, _ = hidden.shape
    at, array = piece
    width, columns = array.shape
    classes = scales.shape[0]
    last_count = len(last)

    def kernel(hidden_ref, total_ref, array_ref, scales_ref, *refs):
        last_refs, out_refs = refs[:last_count], refs[last_count:]
        value = total_ref[0] + jnp.dot(
            hidden_ref[0], array_ref[...], preferred_element_type=jnp.float32
        )
        hidden_two = jnp.tanh(value * scale).astype(jnp.bfloat16)
        out = lax.dot_general(
            jnp.concatenate([ref[...] for ref in last_refs], axis=1), hidden_two,
            (((1,), (1,)), ((), ())), preferred_element_type=jnp.float32,
        )
        out = out * scale * scales_ref[...]
        for i in range(groups):
            @pl.when(pl.program_id(0) == i)
            def _():
                out_refs[i][...] = out

    def whole(shape):
        return pl.BlockSpec(shape, lambda i: (0, 0))

    return launch(
        kernel,
        grid=(groups,),
        in_specs=[
            pl.BlockSpec((1, rows, width), lambda i: (i, 0, at)),
            pl.BlockSpec((1, rows, columns), lambda i: (i, 0, 0)),
            whole((width, columns)),
            whole(scales.shape),
        ]
        + [whole(part.shape) for part in last],
        out_specs=[whole((classes, rows))] * groups,
        out_shape=[jax.ShapeDtypeStruct((classes, rows), jnp.float32)] * groups,
    )(hidden, total, array, scales, *last)


def forward(inputs, first_weight, middle_weight, last_weight, whiten, size, place):
    slots, features, width = first_weight.shape
    parts = size // slots
    units = middle_weight.shape[2]
    y = lax.axis_index(DP) // parts

    def column_block(place_ref, d, e):
        dy, dc = d // parts, d % parts
        at_y, at_c = place_ref[1] // parts, place_ref[1] % parts
        return at_y ^ dy, (at_y ^ dy ^ e) * parts + (at_c ^ dc)

    ds = list(range(size - 1, 0, -1))

    def cut_middle(place_ref, ins, outs):
        if place_ref is None:
            return [(width, slots * width)] * len(ds)
        items = []
        for d, out in zip(ds, outs):
            inward = []
            for e in range(slots):
                slot, at = column_block(place_ref, d, e)
                at = pl.multiple_of(at * width, width)
                inward.append(
                    (ins[0].at[slot, :, pl.ds(at, width)], (slice(None), pl.ds(e * width, width)))
                )
            items.append((inward, [(slice(None), out)]))
        return items

    shape = jax.ShapeDtypeStruct((width, slots * width), middle_weight.dtype)
    cuts = copies(place, [middle_weight], cut_middle, [shape] * len(ds))
    middle_at = {d: swap(cut, DP, size, d) for d, cut in zip(ds, cuts)}

    def own_map(e):
        def index(i, place_ref):
            slot, at = column_block(place_ref, 0, e)
            return slot, 0, at

        return index

    def slot_of(array, dy):
        return lax.dynamic_index_in_dim(array, y ^ dy, 0, keepdims=False)

    def everyone(mine):
        have = dict(zip(range(0, size, parts), mine))
        for bit in bits_of(parts):
            for d, value in list(have.items()):
                have[d ^ bit] = swap(value, DP, size, bit)
        return [have[d] for d in range(size)]

    def far(value_of):
        return [value_of(0)] + [swap(value_of(dy), DP, size, dy * parts) for dy in range(1, slots)]

    every_input = everyone(far(lambda dy: inputs))
    first_all = everyone(far(lambda dy: slot_of(first_weight, dy)))
    last_flipped = jnp.transpose(last_weight, (0, 2, 1))
    last_mine = far(lambda dy: slot_of(last_flipped, dy))
    hidden_one = layer_one(every_input, first_all, features ** (-0.5), size)
    final = parts
    total = layer_two(
        place, hidden_one, (middle_weight, [own_map(e) for e in range(slots)]),
        [(d, middle_at[d]) for d in range(1, size) if d != final],
    )
    blocks = layers_after(
        hidden_one, (final, middle_at[final]), total, last_mine, whiten[:, None], units ** (-0.5)
    )
    received = [block if d == 0 else swap(block, DP, size, d) for d, block in enumerate(blocks)]
    by_slot = [sum(received[dy * parts + dc] for dc in range(parts)) for dy in range(slots)]
    return jnp.concatenate(
        [
            sum(jnp.where(y ^ s == dy, value, 0.0) for dy, value in enumerate(by_slot))
            for s in range(slots)
        ],
        axis=0,
    )


def gram_of(every, observed):
    classes = observed.shape[0]
    counts = [part.shape[0] // classes for part in every]
    ensemble = sum(counts)
    side = -(-(ensemble + 1) // 8) * 8
    count = len(every)

    def kernel(*refs):
        observed_ref, out_ref = refs[count:]
        parts = [(ref[...], n) for ref, n in zip(refs, counts)]
        values = jnp.concatenate(
            [
                jnp.concatenate(
                    [part[j * classes + i][None] for part, n in parts for j in range(n)], axis=0
                )
                for i in range(classes)
            ],
            axis=1,
        )
        seen = jnp.concatenate([observed_ref[i : i + 1, :] for i in range(classes)], axis=1)
        center = jnp.sum(values, axis=0, keepdims=True) / ensemble
        stacked = jnp.concatenate(
            [values - center, jnp.broadcast_to(seen - center, (side - ensemble, seen.shape[1]))],
            axis=0,
        )
        out_ref[...] = lax.dot_general(
            stacked, stacked, (((1,), (1,)), ((), ())),
            precision=precise, preferred_element_type=jnp.float32,
        )

    return launch(
        kernel, out_shape=jax.ShapeDtypeStruct((side, side), jnp.float32)
    )(*every, observed)


def weights_of(every, observed, size):
    ensemble = sum(part.shape[0] for part in every) // observed.shape[0]
    both = gram_of(every, observed)
    bits = bits_of(size)
    for bit in bits[:-1]:
        both = both + swap(both, DP, size, bit)
    other = swap(both, DP, size, bits[-1])

    def kernel(first_ref, second_ref, out_ref):
        total = first_ref[...] + second_ref[...]
        gram_matrix, drive = total[:ensemble, :ensemble], total[:ensemble, ensemble : ensemble + 1]
        row = lax.broadcasted_iota(jnp.int32, (ensemble, ensemble), 0)
        column = lax.broadcasted_iota(jnp.int32, (ensemble, ensemble), 1)
        same = (row == column).astype(jnp.float32)
        system = gram_matrix + ensemble * same
        right = drive - gram_matrix
        at = lax.broadcasted_iota(jnp.int32, (ensemble, 1), 0)
        for j in range(ensemble):
            factor = system[:, j : j + 1] / system[j : j + 1, j : j + 1]
            factor = jnp.where(at == j, 0.0, factor)
            system = system - factor * system[j : j + 1, :]
            right = right - factor * right[j : j + 1, :]
        pivots = jnp.sum(system * same, axis=1, keepdims=True)
        mixing = right / pivots
        out_ref[...] = same + mixing - jnp.sum(mixing, axis=0, keepdims=True) / ensemble

    return launch(
        kernel, out_shape=jax.ShapeDtypeStruct((ensemble, ensemble), jnp.float32)
    )(both, other)


def combine(weights, values, classes):
    slots = weights.shape[1]
    count = len(values)
    width = values[0].shape[1]

    def kernel(weights_ref, *refs):
        out_ref = refs[-1]
        totals, k = [0.0] * slots, 0
        for ref in refs[:count]:
            rows = ref[...].astype(jnp.float32)
            for i in range(0, rows.shape[0], classes):
                for s in range(slots):
                    totals[s] += weights_ref[k, s] * rows[i : i + classes]
                k += 1
        for s in range(slots):
            out_ref[s] = totals[s].astype(out_ref.dtype)

    return launch(
        kernel,
        in_specs=[pl.BlockSpec(memory_space=pltpu.SMEM)]
        + [pl.BlockSpec(memory_space=pltpu.VMEM)] * count,
        out_shape=jax.ShapeDtypeStruct((slots, classes, width), values[0].dtype),
    )(weights, *values)


def relayed(pieces, members):
    out = dict(pieces)
    for k in evens(members):
        if k in pieces:
            out[k] = swap(pieces[k], MEMBER, members, k)
        if k + 1 in pieces:
            near = swap(pieces[k + 1], MEMBER, members, 1)
            out[k + 1] = swap(near, MEMBER, members, k)
    if 1 in pieces:
        out[1] = swap(pieces[1], MEMBER, members, 1)
    return out


def evens(members):
    half = members // 2
    return [half] + [k for k in range(2, members, 2) if k != half]


def held(members):
    return evens(members)[:1] + evens(members)[-1:]


def on_device(
    members, size,
    feature_pool, labels, sample_rows, noise_variance, first_weight, middle_weight, last_weight,
):
    slots = first_weight.shape[0]
    classes_total = noise_variance.shape[0]
    ensemble = members * slots
    here = lax.axis_index(MEMBER)
    place = jnp.stack([here, lax.axis_index(DP)]).astype(jnp.int32)
    whiten = 1.0 / jnp.sqrt(noise_variance)
    inputs = feature_pool[sample_rows]
    classes = labels[sample_rows]
    target = (
        classes[None, :] == jnp.arange(classes_total, dtype=jnp.int32)[:, None]
    ).astype(jnp.float32)
    observed = target * whiten[:, None]

    def blocks(array):
        return array.reshape((slots, members, array.shape[1] // members) + array.shape[2:])

    first_blocks, middle_blocks = blocks(first_weight), blocks(middle_weight)
    rows, columns = middle_blocks.shape[2:]
    tall, wide = first_blocks.shape[2:]
    fits = (
        members >= 8
        and ensemble * GROUP <= WIDEST
        and rows % (2 * GROUP) == 0
        and tall % GROUP == 0
        and tall // GROUP * wide * slots == columns
    )
    scaled = forward(inputs, first_weight, middle_weight, last_weight, whiten, size, place)
    every = gather_members(scaled, members)
    if not fits:
        return plain_update(
            weights_of(every, observed, size), members, first_weight, middle_weight, last_weight
        )

    each = range(members)
    wait = [k + 1 for k in held(members)]
    head = evens(members)[0]
    others = [k for k in each if k != head]
    cut = cut_pieces(place, middle_blocks, first_blocks, [(head, 1, 1)])
    cut += cut_pieces(
        place, middle_blocks, first_blocks,
        [(k, 1, k not in wait) for k in others] + [(k, 0, 1) for k in wait],
    )
    pieces_in = relayed(dict(zip([head] + others, cut)), members)
    late_in = relayed(dict(zip(wait, cut[members:])), members)
    weights = weights_of(every, observed, size)

    half = rows // 2
    strip = slots * half // GROUP
    early_back = relayed(
        dict(
            enumerate(
                update_pieces(
                    weights,
                    [(pieces_in[k], int(k not in wait)) for k in each], slots, half, wide,
                    [(pieces_in[k], strip * (1 + (k not in wait))) for k in each],
                )
            )
        ),
        members,
    )
    late_back = relayed(
        dict(
            enumerate(
                update_pieces(
                    weights,
                    [((late_in if k in wait else pieces_in)[k], 0) for k in each], slots, half, wide,
                )
            )
        ),
        members,
    )
    last_flipped = jnp.transpose(last_weight, (0, 2, 1)).reshape(-1, last_weight.shape[1])
    last_all = gather_members(last_flipped, members)
    new_last = jnp.transpose(combine(weights[:, :slots], last_all, classes_total), (0, 2, 1))

    new_middle, new_first = join_early(
        place, middle_blocks.shape, first_blocks.shape, early_back
    )
    last = evens(members)[-1:] + [k + 1 for k in evens(members)]
    kept = {k: late_back[k] for k in each if k not in last}
    new_middle = join_late(place, new_middle, first_blocks, kept)
    for k in last:
        piece = late_back[k].reshape(slots, 1, half, columns)
        new_middle = lax.dynamic_update_slice(new_middle, piece, (0, here ^ k, half, 0))
    return (
        new_first.reshape(first_weight.shape),
        new_middle.reshape(middle_weight.shape),
        new_last,
    )


def plain_update(weights, members, first_weight, middle_weight, last_weight):
    slots = first_weight.shape[0]
    ensemble = members * slots
    member = jnp.arange(ensemble, dtype=jnp.int32)
    spot = (member // slots ^ lax.axis_index(MEMBER)) * slots + member % slots
    weights = weights[spot][:, spot].T
    upper = weights.astype(jnp.bfloat16)
    lower = (weights - upper.astype(jnp.float32)).astype(jnp.bfloat16)

    def renew(array):
        piece = lax.all_to_all(array, MEMBER, split_axis=1, concat_axis=0, tiled=True)
        flat = piece.reshape(ensemble, -1)
        new = jnp.dot(upper, flat, preferred_element_type=jnp.float32)
        new += jnp.dot(lower, flat, preferred_element_type=jnp.float32)
        new = new.astype(jnp.bfloat16).reshape(piece.shape)
        return lax.all_to_all(new, MEMBER, split_axis=0, concat_axis=1, tiled=True)

    return renew(first_weight), renew(middle_weight), renew(last_weight)


def solution(mesh):
    members, size = mesh.shape[MEMBER], mesh.shape[DP]
    in_specs = (
        P(DP, None),
        P(DP),
        P(DP),
        P(),
        P(MEMBER, None, DP),
        P(MEMBER, DP, None),
        P(MEMBER, DP, None),
    )
    out_specs = (P(MEMBER, None, DP), P(MEMBER, DP, None), P(MEMBER, DP, None))

    def step(*arrays):
        return on_device(members, size, *arrays)

    def run(*arrays):
        mapped = jax.shard_map(
            step, mesh=mesh, in_specs=in_specs, out_specs=out_specs, check_vma=False
        )
        return mapped(*arrays)

    return run
```

```python
import jax
import jax.numpy as jnp
from jax import lax
from jax.experimental import pallas as pl
from jax.experimental.pallas import tpu as pltpu
from jax.sharding import PartitionSpec as P


GROUP = 16
VMEM_GRANT = 65300 * 1024
WIDEST = 256
precise = lax.Precision.HIGHEST
MEMBER, DP = "member", "dp"


def swap(value, axis, size, k):
    return lax.ppermute(value, axis, [(i, i ^ k) for i in range(size)])


def launch(kernel, grant=None, **settings):
    return pl.pallas_call(
        kernel, compiler_params=pltpu.CompilerParams(vmem_limit_bytes=grant), **settings
    )


def bits_of(size):
    return [1 << b for b in range(size.bit_length() - 1)]


def gather_members(value, size):
    have = [value]
    bits = bits_of(size)
    groups = [bits[:1]] + [bits[i : i + 2] for i in range(1, len(bits), 2)]
    for group in groups:
        stack = jnp.concatenate(have, axis=0) if len(have) > 1 else have[0]
        ks = [step * group[0] for step in range(1, 1 << len(group))]
        have = have + [swap(stack, MEMBER, size, k) for k in ks]
    return have


def copies(place, sources, plan, out_shapes, into=()):
    count, kept, results = len(sources), len(into), len(out_shapes)
    shapes = plan(None, None, None)
    total = len(shapes)

    def kernel(place_ref, *refs):
        ins, outs = refs[:count], refs[count + kept : count + kept + results]
        stage, sems = refs[-total - 1 : -1], refs[-1]
        items = [
            (
                [
                    pltpu.make_async_copy(a, stage[i].at[at], sems.at[0, i, j])
                    for j, (a, at) in enumerate(inward)
                ],
                [
                    pltpu.make_async_copy(stage[i].at[at], b, sems.at[1, i, j])
                    for j, (at, b) in enumerate(outward)
                ],
            )
            for i, (inward, outward) in enumerate(plan(place_ref, ins, outs))
        ]
        for inward, _ in items:
            for copy in inward:
                copy.start()
        for inward, outward in items:
            for copy in inward:
                copy.wait()
            for copy in outward:
                copy.start()
        for _, outward in items:
            for copy in outward:
                copy.wait()

    anywhere = pl.BlockSpec(memory_space=pl.ANY)
    return launch(
        kernel,
        in_specs=[pl.BlockSpec(memory_space=pltpu.SMEM)] + [anywhere] * (count + kept),
        out_specs=[anywhere] * results,
        out_shape=out_shapes,
        scratch_shapes=[pltpu.VMEM(shape, jnp.bfloat16) for shape in shapes]
        + [pltpu.SemaphoreType.DMA((2, total, 8))],
        input_output_aliases={1 + count + i: i for i in range(kept)},
    )(place, *sources, *into)


def views(middle, first, k, place_ref, early, late):
    slots, _, rows, _ = middle.shape
    _, _, tall, wide = first.shape
    block, half, found, at = place_ref[0] ^ k, rows // 2, [], 0
    for wanted, start in ((late, half), (early, 0)):
        for s in range(slots if wanted else 0):
            found.append((pl.ds(at, half), middle.at[s, block, start : start + half]))
            at += half
    for s in range(slots if early else 0):
        for h in range(tall // GROUP):
            left = (s * (tall // GROUP) + h) * wide
            found.append(
                (
                    (pl.ds(at, GROUP), pl.ds(left, wide)),
                    first.at[s, block, h * GROUP : (h + 1) * GROUP],
                )
            )
    return found


def piece_shape(middle, early, late):
    slots, _, rows, columns = middle.shape
    return (slots * (rows // 2) * (early + late) + GROUP * early, columns)


def cut_pieces(place, middle, first, wanted):
    shapes = [piece_shape(middle, early, late) for _, early, late in wanted]

    def plan(place_ref, ins, outs):
        if place_ref is None:
            return shapes
        return [
            (
                [(b, at) for at, b in views(*ins, k, place_ref, early, late)],
                [(slice(None), out)],
            )
            for (k, early, late), out in zip(wanted, outs)
        ]

    return list(
        copies(
            place, [middle, first], plan,
            [jax.ShapeDtypeStruct(shape, middle.dtype) for shape in shapes],
        )
    )


def join_early(place, middle_shape, first_shape, pieces):
    def plan(place_ref, ins, outs):
        if place_ref is None:
            return [piece.shape for piece in pieces.values()]
        return [
            ([(ref, slice(None))], views(*outs, k, place_ref, 1, 0)) for k, ref in zip(pieces, ins)
        ]

    shapes = [jax.ShapeDtypeStruct(shape, jnp.bfloat16) for shape in (middle_shape, first_shape)]
    return copies(place, list(pieces.values()), plan, shapes)


def join_late(place, middle, first, pieces):
    def plan(place_ref, ins, outs):
        if place_ref is None:
            return [piece.shape for piece in pieces.values()]
        return [
            ([(ref, slice(None))], views(outs[0], first, k, place_ref, 0, 1))
            for k, ref in zip(pieces, ins)
        ]

    shape = jax.ShapeDtypeStruct(middle.shape, middle.dtype)
    return copies(place, list(pieces.values()), plan, [shape], [middle])[0]


def spread(matrix, rows):
    n = matrix.shape[0]
    wide = n * rows
    pick = (
        lax.broadcasted_iota(jnp.int32, (wide, n), 0) // rows
        == lax.broadcasted_iota(jnp.int32, (wide, n), 1)
    ).astype(jnp.bfloat16)
    tall = lax.dot_general(
        pick, matrix, (((1,), (1,)), ((), ())), preferred_element_type=jnp.float32
    ).astype(jnp.bfloat16)
    full = lax.dot_general(
        tall, pick, (((1,), (1,)), ((), ())), preferred_element_type=jnp.float32
    )
    same = (
        lax.broadcasted_iota(jnp.int32, (wide, wide), 0) % rows
        == lax.broadcasted_iota(jnp.int32, (wide, wide), 1) % rows
    )
    return jnp.where(same, full, 0.0).astype(jnp.bfloat16)


def update_pieces(weights, pieces, slots, rows, block, strips=()):
    count, extra = len(pieces), len(strips)
    columns = pieces[0][0].shape[1]
    wide = count * slots * GROUP
    tall = slots * rows + (GROUP if strips else 0)
    halves = columns // block // slots

    def kernel(weights_ref, *refs):
        ins, refs = refs[:count], refs[count:]
        strip_refs, refs = refs[:extra], refs[extra:]
        outs, (upper_ref, lower_ref) = refs[:count], refs[count:]
        step = pl.program_id(0)

        @pl.when(step == 0)
        def _():
            upper = weights_ref[...].astype(jnp.bfloat16)
            lower = (weights_ref[...] - upper.astype(jnp.float32)).astype(jnp.bfloat16)
            upper_ref[...] = spread(upper, GROUP)
            lower_ref[...] = spread(lower, GROUP)

        def renewed(data):
            data = jnp.concatenate(data, axis=0)
            total = jnp.dot(upper_ref[...], data, preferred_element_type=jnp.float32)
            total += jnp.dot(lower_ref[...], data, preferred_element_type=jnp.float32)
            return total.reshape(count, slots, GROUP, block)

        for first in range(0, rows, GROUP):
            total = renewed(
                [
                    ref[s * rows + first : s * rows + first + GROUP, :]
                    for ref in ins
                    for s in range(slots)
                ]
            ).astype(jnp.bfloat16)
            for i, ref in enumerate(outs):
                for s in range(slots):
                    ref[s * rows + first : s * rows + first + GROUP, :] = total[i, s]
        if strips:
            half = step % halves
            total = renewed(
                [
                    ref[:, pl.ds(pl.multiple_of((s * halves + half) * block, block), block)]
                    for ref in strip_refs
                    for s in range(slots)
                ]
            )
            for i, ref in enumerate(outs):
                mine = total[i, 0]
                for s in range(1, slots):
                    mine = jnp.where(step // halves == s, total[i, s], mine)
                ref[slots * rows : tall, :] = mine.astype(jnp.bfloat16)

    return launch(
        kernel,
        VMEM_GRANT,
        grid=(columns // block,),
        in_specs=[pl.BlockSpec(weights.shape, lambda i: (0, 0))]
        + [pl.BlockSpec((slots * rows, block), lambda i, at=at: (at, i)) for _, at in pieces]
        + [pl.BlockSpec((GROUP, columns), lambda i, at=at: (at, 0)) for _, at in strips],
        out_specs=[pl.BlockSpec((tall, block), lambda i: (0, i))] * count,
        out_shape=[jax.ShapeDtypeStruct((tall, columns), jnp.bfloat16)] * count,
        scratch_shapes=[pltpu.VMEM((wide, wide), jnp.bfloat16)] * 2,
    )(weights, *[array for array, _ in pieces], *[array for array, _ in strips])


def layer_one(inputs, weights, scale, steps):
    rows, features = inputs[0].shape
    width = weights[0].shape[1]
    count, blocks = len(inputs), len(weights)
    tall = rows // steps

    def kernel(*refs):
        out_ref = refs[-1]
        data = jnp.concatenate([ref[...] for ref in refs[:count]], axis=0)
        for j in range(blocks):
            product = jnp.dot(data, refs[count + j][...], preferred_element_type=jnp.float32)
            hidden = jnp.tanh(product * scale).astype(jnp.bfloat16)
            for i in range(count):
                out_ref[i, :, j * width : (j + 1) * width] = hidden[i * tall : (i + 1) * tall]

    return launch(
        kernel,
        grid=(steps,),
        in_specs=[pl.BlockSpec((tall, features), lambda i: (i, 0))] * count
        + [pl.BlockSpec((features, width), lambda i: (0, 0))] * blocks,
        out_specs=pl.BlockSpec((count, tall, blocks * width), lambda i: (0, i, 0)),
        out_shape=jax.ShapeDtypeStruct((count, rows, blocks * width), jnp.bfloat16),
    )(*inputs, *weights)


def layer_two(place, hidden, own, pieces):
    groups, rows, _ = hidden.shape
    width, columns = pieces[0][1].shape
    array, maps = own
    count, own_count = len(pieces), len(maps)

    def kernel(place_ref, *refs):
        hidden_refs, refs = refs[: count + 1], refs[count + 1 :]
        own_refs, piece_refs, out_ref = refs[:own_count], refs[own_count:-1], refs[-1]
        value = jnp.concatenate(
            [
                jnp.dot(hidden_refs[0][0], ref[0], preferred_element_type=jnp.float32)
                for ref in own_refs
            ],
            axis=1,
        )
        for hidden_ref, ref in zip(hidden_refs[1:], piece_refs):
            value += jnp.dot(hidden_ref[0], ref[...], preferred_element_type=jnp.float32)
        out_ref[0] = value

    def column(at):
        return pl.BlockSpec((1, rows, width), lambda i, place_ref: (i, 0, at))

    return launch(
        kernel,
        grid_spec=pltpu.PrefetchScalarGridSpec(
            num_scalar_prefetch=1,
            grid=(groups,),
            in_specs=[column(0)] + [column(at) for at, _ in pieces]
            + [pl.BlockSpec((1, width, columns // own_count), index) for index in maps]
            + [pl.BlockSpec((width, columns), lambda i, place_ref: (0, 0))] * count,
            out_specs=pl.BlockSpec((1, rows, columns), lambda i, place_ref: (i, 0, 0)),
        ),
        out_shape=jax.ShapeDtypeStruct((groups, rows, columns), jnp.float32),
    )(place, *[hidden] * (count + 1), *[array] * own_count, *[value for _, value in pieces])


def layers_after(hidden, piece, total, last, scales, scale):
    groups, rows, _ = hidden.shape
    at, array = piece
    width, columns = array.shape
    classes = scales.shape[0]
    last_count = len(last)

    def kernel(hidden_ref, total_ref, array_ref, scales_ref, *refs):
        last_refs, out_refs = refs[:last_count], refs[last_count:]
        value = total_ref[0] + jnp.dot(
            hidden_ref[0], array_ref[...], preferred_element_type=jnp.float32
        )
        hidden_two = jnp.tanh(value * scale).astype(jnp.bfloat16)
        out = lax.dot_general(
            jnp.concatenate([ref[...] for ref in last_refs], axis=1), hidden_two,
            (((1,), (1,)), ((), ())), preferred_element_type=jnp.float32,
        )
        out = out * scale * scales_ref[...]
        for i in range(groups):
            @pl.when(pl.program_id(0) == i)
            def _():
                out_refs[i][...] = out

    def whole(shape):
        return pl.BlockSpec(shape, lambda i: (0, 0))

    return launch(
        kernel,
        grid=(groups,),
        in_specs=[
            pl.BlockSpec((1, rows, width), lambda i: (i, 0, at)),
            pl.BlockSpec((1, rows, columns), lambda i: (i, 0, 0)),
            whole((width, columns)),
            whole(scales.shape),
        ]
        + [whole(part.shape) for part in last],
        out_specs=[whole((classes, rows))] * groups,
        out_shape=[jax.ShapeDtypeStruct((classes, rows), jnp.float32)] * groups,
    )(hidden, total, array, scales, *last)


def forward(inputs, first_weight, middle_weight, last_weight, whiten, size, place):
    slots, features, width = first_weight.shape
    parts = size // slots
    units = middle_weight.shape[2]
    y = lax.axis_index(DP) // parts

    def column_block(place_ref, d, e):
        dy, dc = d // parts, d % parts
        at_y, at_c = place_ref[1] // parts, place_ref[1] % parts
        return at_y ^ dy, (at_y ^ dy ^ e) * parts + (at_c ^ dc)

    ds = list(range(size - 1, 0, -1))

    def cut_middle(place_ref, ins, outs):
        if place_ref is None:
            return [(width, slots * width)] * len(ds)
        items = []
        for d, out in zip(ds, outs):
            inward = []
            for e in range(slots):
                slot, at = column_block(place_ref, d, e)
                at = pl.multiple_of(at * width, width)
                inward.append(
                    (ins[0].at[slot, :, pl.ds(at, width)], (slice(None), pl.ds(e * width, width)))
                )
            items.append((inward, [(slice(None), out)]))
        return items

    shape = jax.ShapeDtypeStruct((width, slots * width), middle_weight.dtype)
    cuts = copies(place, [middle_weight], cut_middle, [shape] * len(ds))
    middle_at = {d: swap(cut, DP, size, d) for d, cut in zip(ds, cuts)}

    def own_map(e):
        def index(i, place_ref):
            slot, at = column_block(place_ref, 0, e)
            return slot, 0, at

        return index

    def slot_of(array, dy):
        return lax.dynamic_index_in_dim(array, y ^ dy, 0, keepdims=False)

    def everyone(mine):
        have = dict(zip(range(0, size, parts), mine))
        for bit in bits_of(parts):
            for d, value in list(have.items()):
                have[d ^ bit] = swap(value, DP, size, bit)
        return [have[d] for d in range(size)]

    def far(value_of):
        return [value_of(0)] + [swap(value_of(dy), DP, size, dy * parts) for dy in range(1, slots)]

    every_input = everyone(far(lambda dy: inputs))
    first_all = everyone(far(lambda dy: slot_of(first_weight, dy)))
    last_flipped = jnp.transpose(last_weight, (0, 2, 1))
    last_mine = far(lambda dy: slot_of(last_flipped, dy))
    hidden_one = layer_one(every_input, first_all, features ** (-0.5), size)
    final = parts
    total = layer_two(
        place, hidden_one, (middle_weight, [own_map(e) for e in range(slots)]),
        [(d, middle_at[d]) for d in range(1, size) if d != final],
    )
    blocks = layers_after(
        hidden_one, (final, middle_at[final]), total, last_mine, whiten[:, None], units ** (-0.5)
    )
    received = [block if d == 0 else swap(block, DP, size, d) for d, block in enumerate(blocks)]
    by_slot = [sum(received[dy * parts + dc] for dc in range(parts)) for dy in range(slots)]
    return jnp.concatenate(
        [
            sum(jnp.where(y ^ s == dy, value, 0.0) for dy, value in enumerate(by_slot))
            for s in range(slots)
        ],
        axis=0,
    )


def gram_of(every, observed):
    classes = observed.shape[0]
    counts = [part.shape[0] // classes for part in every]
    ensemble = sum(counts)
    side = -(-(ensemble + 1) // 8) * 8
    count = len(every)

    def kernel(*refs):
        observed_ref, out_ref = refs[count:]
        parts = [(ref[...], n) for ref, n in zip(refs[:count], counts)]
        values = jnp.concatenate(
            [
                jnp.concatenate(
                    [part[j * classes + i][None] for part, n in parts for j in range(n)], axis=0
                )
                for i in range(classes)
            ],
            axis=1,
        )
        seen = jnp.concatenate([observed_ref[i : i + 1, :] for i in range(classes)], axis=1)
        center = jnp.sum(values, axis=0, keepdims=True) / ensemble
        stacked = jnp.concatenate(
            [values - center, jnp.broadcast_to(seen - center, (side - ensemble, seen.shape[1]))],
            axis=0,
        )
        out_ref[...] = lax.dot_general(
            stacked, stacked, (((1,), (1,)), ((), ())),
            precision=precise, preferred_element_type=jnp.float32,
        )

    return launch(
        kernel,
        in_specs=[pl.BlockSpec(memory_space=pltpu.VMEM)] * (count + 1),
        out_shape=jax.ShapeDtypeStruct((side, side), jnp.float32),
    )(*every, observed)


def weights_of(every, observed, size):
    ensemble = sum(part.shape[0] for part in every) // observed.shape[0]
    both = gram_of(every, observed)
    bits = bits_of(size)
    for bit in bits[:-1]:
        both = both + swap(both, DP, size, bit)
    other = swap(both, DP, size, bits[-1])

    def kernel(first_ref, second_ref, out_ref):
        total = first_ref[...] + second_ref[...]
        gram_matrix, drive = total[:ensemble, :ensemble], total[:ensemble, ensemble : ensemble + 1]
        row = lax.broadcasted_iota(jnp.int32, (ensemble, ensemble), 0)
        column = lax.broadcasted_iota(jnp.int32, (ensemble, ensemble), 1)
        same = (row == column).astype(jnp.float32)
        system = gram_matrix + ensemble * same
        right = drive - gram_matrix
        at = lax.broadcasted_iota(jnp.int32, (ensemble, 1), 0)
        for j in range(ensemble):
            factor = system[:, j : j + 1] / system[j : j + 1, j : j + 1]
            factor = jnp.where(at == j, 0.0, factor)
            system = system - factor * system[j : j + 1, :]
            right = right - factor * right[j : j + 1, :]
        pivots = jnp.sum(system * same, axis=1, keepdims=True)
        mixing = right / pivots
        out_ref[...] = same + mixing - jnp.sum(mixing, axis=0, keepdims=True) / ensemble

    return launch(
        kernel,
        VMEM_GRANT,
        in_specs=[pl.BlockSpec(memory_space=pltpu.VMEM)] * 2,
        out_shape=jax.ShapeDtypeStruct((ensemble, ensemble), jnp.float32),
    )(both, other)


def doubled(value, size):
    have, order = [value], [0]
    for bit in doubling(size):
        stack = jnp.concatenate(have, axis=0) if len(have) > 1 else have[0]
        have = have + [swap(stack, MEMBER, size, bit)]
        order = order + [k ^ bit for k in order]
    return have, order


def doubling(size):
    bits = bits_of(size)
    return bits[:1] + bits[:0:-1]


def combine(weights, values, order, classes):
    slots = weights.shape[1]
    count = len(values)
    width = values[0].shape[1]

    def kernel(weights_ref, *refs):
        out_ref = refs[-1]
        totals, k = [0.0] * slots, 0
        for ref in refs[:count]:
            rows = ref[...].astype(jnp.float32)
            for i in range(0, rows.shape[0], classes):
                at = order[k // slots] * slots + k % slots
                for s in range(slots):
                    totals[s] += weights_ref[at, s] * rows[i : i + classes]
                k += 1
        for s in range(slots):
            out_ref[s] = totals[s].astype(out_ref.dtype)

    return launch(
        kernel,
        in_specs=[pl.BlockSpec(memory_space=pltpu.SMEM)]
        + [pl.BlockSpec(memory_space=pltpu.VMEM)] * count,
        out_shape=jax.ShapeDtypeStruct((slots, classes, width), values[0].dtype),
    )(weights, *values)


def relayed(pieces, members):
    out = dict(pieces)
    for k in evens(members):
        if k in pieces:
            out[k] = swap(pieces[k], MEMBER, members, k)
        if k + 1 in pieces:
            near = swap(pieces[k + 1], MEMBER, members, 1)
            out[k + 1] = swap(near, MEMBER, members, k)
    if 1 in pieces:
        out[1] = swap(pieces[1], MEMBER, members, 1)
    return out


def evens(members):
    return list(range(2, members, 2))


def held(members):
    return [members // 2, members - 2]


def on_device(
    members, size,
    feature_pool, labels, sample_rows, noise_variance, first_weight, middle_weight, last_weight,
):
    slots = first_weight.shape[0]
    classes_total = noise_variance.shape[0]
    ensemble = members * slots
    here = lax.axis_index(MEMBER)
    place = jnp.stack([here, lax.axis_index(DP)]).astype(jnp.int32)
    whiten = 1.0 / jnp.sqrt(noise_variance)
    inputs = feature_pool[sample_rows]
    classes = labels[sample_rows]
    target = (
        classes[None, :] == jnp.arange(classes_total, dtype=jnp.int32)[:, None]
    ).astype(jnp.float32)
    observed = target * whiten[:, None]

    def blocks(array):
        return array.reshape((slots, members, array.shape[1] // members) + array.shape[2:])

    first_blocks, middle_blocks = blocks(first_weight), blocks(middle_weight)
    rows, columns = middle_blocks.shape[2:]
    tall, wide = first_blocks.shape[2:]
    fits = (
        members >= 8
        and ensemble * GROUP <= WIDEST
        and rows % (2 * GROUP) == 0
        and tall % GROUP == 0
        and tall // GROUP * wide * slots == columns
    )
    scaled = forward(inputs, first_weight, middle_weight, last_weight, whiten, size, place)
    every = gather_members(scaled, members)
    if not fits:
        return plain_update(
            weights_of(every, observed, size), members, first_weight, middle_weight, last_weight
        )

    each = range(members)
    wait = [k + 1 for k in held(members)]
    head = held(members)[0]
    others = [k for k in each if k != head]
    cut = cut_pieces(place, middle_blocks, first_blocks, [(head, 1, 1)])
    cut += cut_pieces(
        place, middle_blocks, first_blocks,
        [(k, 1, k not in wait) for k in others] + [(k, 0, 1) for k in wait],
    )
    pieces_in = relayed(dict(zip([head] + others, cut)), members)
    late_in = relayed(dict(zip(wait, cut[members:])), members)
    weights = weights_of(every, observed, size)

    half = rows // 2
    strip = slots * half // GROUP
    early_back = relayed(
        dict(
            enumerate(
                update_pieces(
                    weights,
                    [(pieces_in[k], int(k not in wait)) for k in each], slots, half, wide,
                    [(pieces_in[k], strip * (1 + (k not in wait))) for k in each],
                )
            )
        ),
        members,
    )
    late_back = relayed(
        dict(
            enumerate(
                update_pieces(
                    weights,
                    [((late_in if k in wait else pieces_in)[k], 0) for k in each], slots, half, wide,
                )
            )
        ),
        members,
    )
    last_flipped = jnp.transpose(last_weight, (0, 2, 1)).reshape(-1, last_weight.shape[1])
    last_all, order = doubled(last_flipped, members)
    new_last = jnp.transpose(
        combine(weights[:, :slots], last_all, order, classes_total), (0, 2, 1)
    )

    new_middle, new_first = join_early(
        place, middle_blocks.shape, first_blocks.shape, early_back
    )
    last = evens(members)[-1:] + [k + 1 for k in evens(members)]
    kept = {k: late_back[k] for k in each if k not in last}
    new_middle = join_late(place, new_middle, first_blocks, kept)
    for k in last:
        piece = late_back[k].reshape(slots, 1, half, columns)
        new_middle = lax.dynamic_update_slice(new_middle, piece, (0, here ^ k, half, 0))
    return (
        new_first.reshape(first_weight.shape),
        new_middle.reshape(middle_weight.shape),
        new_last,
    )


def plain_update(weights, members, first_weight, middle_weight, last_weight):
    slots = first_weight.shape[0]
    ensemble = members * slots
    member = jnp.arange(ensemble, dtype=jnp.int32)
    spot = (member // slots ^ lax.axis_index(MEMBER)) * slots + member % slots
    weights = weights[spot][:, spot].T
    upper = weights.astype(jnp.bfloat16)
    lower = (weights - upper.astype(jnp.float32)).astype(jnp.bfloat16)

    def renew(array):
        piece = lax.all_to_all(array, MEMBER, split_axis=1, concat_axis=0, tiled=True)
        flat = piece.reshape(ensemble, -1)
        new = jnp.dot(upper, flat, preferred_element_type=jnp.float32)
        new += jnp.dot(lower, flat, preferred_element_type=jnp.float32)
        new = new.astype(jnp.bfloat16).reshape(piece.shape)
        return lax.all_to_all(new, MEMBER, split_axis=0, concat_axis=1, tiled=True)

    return renew(first_weight), renew(middle_weight), renew(last_weight)


def solution(mesh):
    members, size = mesh.shape[MEMBER], mesh.shape[DP]
    in_specs = (
        P(DP, None),
        P(DP),
        P(DP),
        P(),
        P(MEMBER, None, DP),
        P(MEMBER, DP, None),
        P(MEMBER, DP, None),
    )
    out_specs = (P(MEMBER, None, DP), P(MEMBER, DP, None), P(MEMBER, DP, None))

    def step(*arrays):
        return on_device(members, size, *arrays)

    def run(*arrays):
        mapped = jax.shard_map(
            step, mesh=mesh, in_specs=in_specs, out_specs=out_specs, check_vma=False
        )
        return mapped(*arrays)

    return run
```
